32 devices in a mesh: seq: 2 (over core), head: 4 (over y, x), batch: 4 (over z).
Axes of the slice: x: 2, y: 2, z: 4, core: 2. Of those that a mesh axis runs over, the one named last changes fastest.
Arguments:
- block_in: bfloat16 [4, 1024, 768], P('batch', 'seq'), may hold values from -6 to 6
- out_grad: bfloat16 [4, 1024, 768], P('batch', 'seq'), may hold values from -6 to 6
- norm_gain: float32 [768], replicated, may hold values from 0.5 to 1.5
- in_proj: float32 [2, 768, 1536], P(None, ('seq', 'batch'), 'head'), may hold values from -0.21875 to 0.21875
- bc_proj: float32 [768, 256], P('head', ('seq', 'batch')), may hold values from -0.21875 to 0.21875
- dt_proj: float32 [768, 24], P(('seq', 'batch'), 'head'), may hold values from -0.21875 to 0.21875
- out_proj: float32 [1536, 768], P('head', ('seq', 'batch')), may hold values from -0.15625 to 0.15625
- chan_params: float32 [6, 1536], P(None, 'head'), may hold values from -0.6 to 1.5, as said below
- head_params: float32 [3, 24], P(None, 'head'), may hold values from -10 to 1.5, as said below
- bc_conv: float32 [5, 256], replicated, may hold values from -0.6 to 0.6, as said below
- first_norm_gain: float32 [768], replicated, may hold values from -60 to 60
- second_norm_gain: float32 [768], replicated, may hold values from 100 to 2000
- first_in_proj: float32 [2, 768, 1536], P(None, ('seq', 'batch'), 'head'), may hold values from -60 to 60
- second_in_proj: float32 [2, 768, 1536], P(None, ('seq', 'batch'), 'head'), may hold values from 100 to 2000
- first_bc_proj: float32 [768, 256], P('head', ('seq', 'batch')), may hold values from -60 to 60
- second_bc_proj: float32 [768, 256], P('head', ('seq', 'batch')), may hold values from 100 to 2000
- first_dt_proj: float32 [768, 24], P(('seq', 'batch'), 'head'), may hold values from -60 to 60
- second_dt_proj: float32 [768, 24], P(('seq', 'batch'), 'head'), may hold values from 100 to 2000
- first_out_proj: float32 [1536, 768], P('head', ('seq', 'batch')), may hold values from -60 to 60
- second_out_proj: float32 [1536, 768], P('head', ('seq', 'batch')), may hold values from 100 to 2000
- first_chan_params: float32 [6, 1536], P(None, 'head'), may hold values from -60 to 60
- second_chan_params: float32 [6, 1536], P(None, 'head'), may hold values from 100 to 2000
- first_head_params: float32 [3, 24], P(None, 'head'), may hold values from -60 to 60
- second_head_params: float32 [3, 24], P(None, 'head'), may hold values from 100 to 2000
- first_bc_conv: float32 [5, 256], replicated, may hold values from -60 to 60
- second_bc_conv: float32 [5, 256], replicated, may hold values from 100 to 2000
Outputs:
- block_out: bfloat16 [4, 1024, 768], P('batch', 'seq')
- in_grad: float32 [4, 1024, 768], P('batch', 'seq')
- grad_norm_gain: float32 [768], replicated
- grad_in_proj: float32 [2, 768, 1536], P(None, ('seq', 'batch'), 'head')
- grad_bc_proj: float32 [768, 256], P('head', ('seq', 'batch'))
- grad_dt_proj: float32 [768, 24], P(('seq', 'batch'), 'head')
- grad_out_proj: float32 [1536, 768], P('head', ('seq', 'batch'))
- grad_chan_params: float32 [6, 1536], P(None, 'head')
- grad_head_params: float32 [3, 24], P(None, 'head')
- grad_bc_conv: float32 [5, 256], replicated
- new_norm_gain: float32 [768], replicated
- new_in_proj: float32 [2, 768, 1536], P(None, ('seq', 'batch'), 'head')
- new_bc_proj: float32 [768, 256], P('head', ('seq', 'batch'))
- new_dt_proj: float32 [768, 24], P(('seq', 'batch'), 'head')
- new_out_proj: float32 [1536, 768], P('head', ('seq', 'batch'))
- new_chan_params: float32 [6, 1536], P(None, 'head')
- new_head_params: float32 [3, 24], P(None, 'head')
- new_bc_conv: float32 [5, 256], replicated
- new_first_norm_gain: float32 [768], replicated
- new_second_norm_gain: float32 [768], replicated
- new_first_in_proj: float32 [2, 768, 1536], P(None, ('seq', 'batch'), 'head')
- new_second_in_proj: float32 [2, 768, 1536], P(None, ('seq', 'batch'), 'head')
- new_first_bc_proj: float32 [768, 256], P('head', ('seq', 'batch'))
- new_second_bc_proj: float32 [768, 256], P('head', ('seq', 'batch'))
- new_first_dt_proj: float32 [768, 24], P(('seq', 'batch'), 'head')
- new_second_dt_proj: float32 [768, 24], P(('seq', 'batch'), 'head')
- new_first_out_proj: float32 [1536, 768], P('head', ('seq', 'batch'))
- new_second_out_proj: float32 [1536, 768], P('head', ('seq', 'batch'))
- new_first_chan_params: float32 [6, 1536], P(None, 'head')
- new_second_chan_params: float32 [6, 1536], P(None, 'head')
- new_first_head_params: float32 [3, 24], P(None, 'head')
- new_second_head_params: float32 [3, 24], P(None, 'head')
- new_first_bc_conv: float32 [5, 256], replicated
- new_second_bc_conv: float32 [5, 256], replicated
The draws below stay inside these ranges and needn't reach their ends.
Inputs may be any that keep to these rules, and one draw needn't show every extreme that they name: `head_params`: row 0 holds the time-step biases, row 1 the logarithms of the decay rates, row 2 the skip gains. `chan_params`: rows 0 to 3 hold the taps, row 4 the bias, row 5 the gated-norm gain. `bc_conv`: rows 0 to 3 hold the taps, row 4 the bias.
All inputs are finite; a program needn't handle non-finite values.
Results may differ from the reference program's by a relative error of at most 0.012.
The reference program's roundings to bfloat16 on the way count: a program that leaves them out, or rounds other values in their place, can miss the bound.
Values may be sent and summed in bfloat16 or wider, within the bound.
A program may use at most 128 MiB of HBM per device.

```python
import math
import jax
import jax.numpy as jnp
from jax import lax

D = 768
H = 24
P_SIZE = 64
N = 128
K = 4
Q = 256
DI = 1536
LENGTH = 1024
SEQS = 4


def conv_table(key, channels, with_gain):
    split_keys = jax.random.split(key, 3)
    tap_rows = jax.random.uniform(split_keys[0], (K, channels), jnp.float32, -0.6, 0.6)
    bias_row = jax.random.uniform(split_keys[1], (1, channels), jnp.float32, -0.5, 0.5)
    table_rows = [tap_rows, bias_row]
    if with_gain:
        table_rows.append(jax.random.uniform(split_keys[2], (1, channels), jnp.float32, 0.5, 1.5))
    return jnp.concatenate(table_rows, 0)


def draw_chan_params(key, part):
    return conv_table(jax.random.fold_in(key, 11), DI, True)


def draw_bc_conv(key, part):
    return conv_table(jax.random.fold_in(key, 13), 2 * N, False)


def draw_head_params(key, part):
    split_keys = jax.random.split(jax.random.fold_in(key, 17), 3)
    step_bias = jax.random.uniform(split_keys[0], (H,), jnp.float32, -4.0, -2.0)
    log_rate = jax.random.uniform(split_keys[1], (H,), jnp.float32, -9.5, -0.5)
    skip_gain = jax.random.uniform(split_keys[2], (H,), jnp.float32, 0.5, 1.5)
    return jnp.stack([step_bias, log_rate, skip_gain])


def steps_of(own_key, dims, cuts, low, largest):
    level, own = 1.0, jax.random.fold_in(own_key, 6)
    for axis_at, shards_of in cuts:
        heights = jnp.exp(jax.random.uniform(jax.random.fold_in(own, axis_at), (shards_of,), jnp.float32, low / len(cuts), largest / len(cuts)))
        level = level * jnp.repeat(heights, dims[axis_at] // shards_of).reshape([-1 if axis == axis_at else 1 for axis in range(len(dims))])
    return level


def normal_values(key, dims, scale, bound, cuts=(), kind=jnp.bfloat16):
    gain = steps_of(key, dims, cuts, -0.22, 0.18) if cuts else 1.0
    drawn = jax.random.normal(key, dims, jnp.float32) * scale * gain
    return jnp.minimum(jnp.maximum(drawn, -bound), bound).astype(kind)


def setup_inputs(seed: int = 0) -> dict:
    key_list = jax.random.split(jax.random.key(seed), 27)
    block_in = normal_values(key_list[0], (SEQS, LENGTH, D), 1.0, 6.0, ((0, 4), (1, 2)))
    out_grad = normal_values(key_list[1], (SEQS, LENGTH, D), 1.0, 6.0, ((0, 4), (1, 2)))
    norm_gain = jnp.clip(1.0 + 0.1 * jax.random.normal(key_list[2], (D,), jnp.float32), 0.5, 1.5)
    in_proj = normal_values(key_list[3], (2, D, DI), D ** -0.5, 0.21875, ((1, 8), (2, 4)), jnp.float32)
    bc_proj = normal_values(key_list[4], (D, 2 * N), D ** -0.5, 0.21875, ((0, 4), (1, 8)), jnp.float32)
    dt_proj = normal_values(key_list[5], (D, H), D ** -0.5, 0.21875, ((0, 8), (1, 4)), jnp.float32)
    out_proj = normal_values(key_list[6], (DI, D), DI ** -0.5, 0.15625, ((0, 4), (1, 8)), jnp.float32)
    chan_params = draw_chan_params(jax.random.fold_in(key_list[26], 71), 0)
    head_params = draw_head_params(jax.random.fold_in(key_list[26], 71), 0)
    bc_conv = draw_bc_conv(jax.random.fold_in(key_list[26], 71), 0)
    first_norm_gain = normal_values(key_list[10], (D,), 10.0, 60.0, (), jnp.float32)
    second_norm_gain = jnp.clip(jnp.exp(jax.random.uniform(key_list[11], (D,), jnp.float32, math.log(100.0), math.log(2000.0))), 100.0, 2000.0)
    first_in_proj = normal_values(key_list[12], (2, D, DI), 10.0, 60.0, ((1, 8), (2, 4)), jnp.float32)
    second_in_proj = jnp.clip(jnp.exp(math.log(2000.0) - 2.9957323 * jax.random.uniform(key_list[13], (2, D, DI), jnp.float32) ** steps_of(key_list[13], (2, D, DI), ((1, 8), (2, 4)), -0.2, 0.2)), 100.0, 2000.0)
    first_bc_proj = normal_values(key_list[14], (D, 2 * N), 10.0, 60.0, ((0, 4), (1, 8)), jnp.float32)
    second_bc_proj = jnp.clip(jnp.exp(math.log(2000.0) - 2.9957323 * jax.random.uniform(key_list[15], (D, 2 * N), jnp.float32) ** steps_of(key_list[15], (D, 2 * N), ((0, 4), (1, 8)), -0.2, 0.2)), 100.0, 2000.0)
    first_dt_proj = normal_values(key_list[16], (D, H), 10.0, 60.0, ((0, 8), (1, 4)), jnp.float32)
    second_dt_proj = jnp.clip(jnp.exp(math.log(2000.0) - 2.9957323 * jax.random.uniform(key_list[17], (D, H), jnp.float32) ** steps_of(key_list[17], (D, H), ((0, 8), (1, 4)), -0.2, 0.2)), 100.0, 2000.0)
    first_out_proj = normal_values(key_list[18], (DI, D), 10.0, 60.0, ((0, 4), (1, 8)), jnp.float32)
    second_out_proj = jnp.clip(jnp.exp(math.log(2000.0) - 2.9957323 * jax.random.uniform(key_list[19], (DI, D), jnp.float32) ** steps_of(key_list[19], (DI, D), ((0, 4), (1, 8)), -0.2, 0.2)), 100.0, 2000.0)
    first_chan_params = normal_values(key_list[20], (K + 2, DI), 10.0, 60.0, ((1, 4),), jnp.float32)
    second_chan_params = jnp.clip(jnp.exp(math.log(2000.0) - 2.9957323 * jax.random.uniform(key_list[21], (K + 2, DI), jnp.float32) ** steps_of(key_list[21], (K + 2, DI), ((1, 4),), -0.2, 0.2)), 100.0, 2000.0)
    first_head_params = normal_values(key_list[22], (3, H), 10.0, 60.0, ((1, 4),), jnp.float32)
    second_head_params = jnp.clip(jnp.exp(math.log(2000.0) - 2.9957323 * jax.random.uniform(key_list[23], (3, H), jnp.float32) ** steps_of(key_list[23], (3, H), ((1, 4),), -0.2, 0.2)), 100.0, 2000.0)
    first_bc_conv = normal_values(key_list[24], (K + 1, 2 * N), 10.0, 60.0, (), jnp.float32)
    second_bc_conv = jnp.clip(jnp.exp(jax.random.uniform(key_list[25], (K + 1, 2 * N), jnp.float32, math.log(100.0), math.log(2000.0))), 100.0, 2000.0)
    return {"block_in": block_in, "out_grad": out_grad, "norm_gain": norm_gain, "in_proj": in_proj, "bc_proj": bc_proj, "dt_proj": dt_proj, "out_proj": out_proj, "chan_params": chan_params, "head_params": head_params, "bc_conv": bc_conv, "first_norm_gain": first_norm_gain, "second_norm_gain": second_norm_gain, "first_in_proj": first_in_proj, "second_in_proj": second_in_proj, "first_bc_proj": first_bc_proj, "second_bc_proj": second_bc_proj, "first_dt_proj": first_dt_proj, "second_dt_proj": second_dt_proj, "first_out_proj": first_out_proj, "second_out_proj": second_out_proj, "first_chan_params": first_chan_params, "second_chan_params": second_chan_params, "first_head_params": first_head_params, "second_head_params": second_head_params, "first_bc_conv": first_bc_conv, "second_bc_conv": second_bc_conv}


eps_norm = 1e-05
beta_one = 0.9
beta_two = 0.95
adam_eps = 1e-08
rate_matrix = 0.01
rate_vector = 0.1
decay_matrix = 0.1
adam_step = 3.0
highest = lax.Precision.HIGHEST

def rms_forward(values, gain_vec):
    scaling = lax.rsqrt(lax.optimization_barrier(jnp.mean(values * values, axis=-1, keepdims=True)) + eps_norm)
    return values * scaling * gain_vec[None, :]

def conv_forward(padded, tap_rows, bias_row):
    width_k = tap_rows.shape[0]
    length = padded.shape[0] - width_k + 1
    summed = jnp.zeros((length, padded.shape[1]), jnp.float32) + bias_row[None, :]
    for offset in range(width_k):
        summed = summed + tap_rows[offset][None, :] * padded[offset:offset + length]
    return jax.nn.silu(summed)

def block_step(carry_state, inputs):
    inner_x, steps_dt, steps_log, b_rows, c_rows = inputs
    cumulative = jnp.cumsum(steps_log, axis=0)
    length = cumulative.shape[0]
    causal = (jnp.arange(length)[:, None] >= jnp.arange(length)[None, :])[:, :, None]
    spread = cumulative[:, None, :] - cumulative[None, :, :]
    decays = jnp.where(causal, jnp.exp(jnp.where(causal, spread, 0.0)), 0.0)
    scores = jnp.dot(c_rows, b_rows.T, precision=highest)
    mixing = scores[:, :, None] * decays * steps_dt[None, :, :]
    in_block = jnp.einsum('tjh,jhp->thp', mixing, inner_x, precision=highest)
    from_state = jnp.einsum('hpn,tn->thp', carry_state, c_rows, precision=highest) * jnp.exp(cumulative)[:, :, None]
    tail_weight = jnp.exp(cumulative[-1][None, :] - cumulative) * steps_dt
    carried = jnp.exp(cumulative[-1])[:, None, None] * carry_state + jnp.einsum('jh,jhp,jn->hpn', tail_weight, inner_x, b_rows, precision=highest)
    return (carried, in_block + from_state)

def ssd_scan(inner_x, steps_dt, steps_log, b_rows, c_rows, start_state):
    block_count = inner_x.shape[0] // Q
    head_count = inner_x.shape[1]
    blocks = (inner_x.reshape(block_count, Q, head_count, inner_x.shape[2]), steps_dt.reshape(block_count, Q, head_count), steps_log.reshape(block_count, Q, head_count), b_rows.reshape(block_count, Q, b_rows.shape[1]), c_rows.reshape(block_count, Q, c_rows.shape[1]))
    end_state, outputs = lax.scan(block_step, start_state, blocks)
    return (outputs.reshape(inner_x.shape), end_state)

def middle(gate_pre, inner_pre, bc_pre, step_raw, chan_params, head_params, bc_conv):
    tokens = gate_pre.shape[0]
    conv_inner = conv_forward(jnp.pad(inner_pre, ((K - 1, 0), (0, 0))), chan_params[:K], chan_params[K])
    conv_bc = conv_forward(jnp.pad(bc_pre, ((K - 1, 0), (0, 0))), bc_conv[:K], bc_conv[K])
    steps_dt = jax.nn.softplus(step_raw + head_params[0][None, :])
    steps_log = -jnp.exp(head_params[1])[None, :] * steps_dt
    inner_x = conv_inner.reshape(tokens, H, P_SIZE)
    ssd_out, end_state = ssd_scan(inner_x, steps_dt, steps_log, conv_bc[:, :N], conv_bc[:, N:], jnp.zeros((H, P_SIZE, N), jnp.float32))
    mixed_rows = (ssd_out + head_params[2][None, :, None] * inner_x).reshape(tokens, DI)
    gated_rows = mixed_rows * jax.nn.silu(gate_pre)
    scaling = lax.rsqrt(lax.optimization_barrier(jnp.mean(gated_rows * gated_rows, axis=-1, keepdims=True)) + eps_norm)
    return gated_rows * scaling * chan_params[K + 1][None, :]

def one_sequence(block_rows, grad_rows, weights_b, small_params):
    zx_b, bc_b, dt_b, out_b = weights_b
    norm_gain, chan_params, head_params, bc_conv = small_params
    block_f = block_rows.astype(jnp.float32)
    normed, norm_back = jax.vjp(rms_forward, block_f, norm_gain)
    normed_b = normed.astype(jnp.bfloat16)
    gate_pre = jnp.dot(normed_b, zx_b[0], preferred_element_type=jnp.float32)
    inner_pre = jnp.dot(normed_b, zx_b[1], preferred_element_type=jnp.float32)
    bc_pre = jnp.dot(normed_b, bc_b, preferred_element_type=jnp.float32)
    step_raw = jnp.dot(normed_b, dt_b, preferred_element_type=jnp.float32)
    mixed_norm, mid_back = jax.vjp(middle, gate_pre, inner_pre, bc_pre, step_raw, chan_params, head_params, bc_conv)
    mixed_b = mixed_norm.astype(jnp.bfloat16)
    out_rows = (block_f + jnp.dot(mixed_b, out_b, preferred_element_type=jnp.float32)).astype(jnp.bfloat16)
    grad_mixed = jnp.dot(grad_rows, out_b.T, preferred_element_type=jnp.float32)
    grad_out_proj = jnp.dot(mixed_b.T, grad_rows, preferred_element_type=jnp.float32)
    grad_gate, grad_inner, grad_bc, grad_step, grad_chan, grad_head, grad_bcconv = mid_back(grad_mixed)
    grad_gate_b = grad_gate.astype(jnp.bfloat16)
    grad_inner_b = grad_inner.astype(jnp.bfloat16)
    grad_bc_b = grad_bc.astype(jnp.bfloat16)
    grad_step_b = grad_step.astype(jnp.bfloat16)
    grad_in_proj = jnp.stack([jnp.dot(normed_b.T, grad_gate_b, preferred_element_type=jnp.float32), jnp.dot(normed_b.T, grad_inner_b, preferred_element_type=jnp.float32)])
    grad_bc_proj = jnp.dot(normed_b.T, grad_bc_b, preferred_element_type=jnp.float32)
    grad_dt_proj = jnp.dot(normed_b.T, grad_step_b, preferred_element_type=jnp.float32)
    grad_normed = jnp.dot(grad_gate_b, zx_b[0].T, preferred_element_type=jnp.float32) + jnp.dot(grad_inner_b, zx_b[1].T, preferred_element_type=jnp.float32) + jnp.dot(grad_bc_b, bc_b.T, preferred_element_type=jnp.float32) + jnp.dot(grad_step_b, dt_b.T, preferred_element_type=jnp.float32)
    grad_block, grad_gain = norm_back(grad_normed)
    in_rows = grad_rows.astype(jnp.float32) + grad_block
    grads = (grad_gain, grad_in_proj, grad_bc_proj, grad_dt_proj, grad_out_proj, grad_chan, grad_head, grad_bcconv)
    return (out_rows, in_rows, grads)

def adamw(weight, grad_sum, moment_one, moment_two, step_rate, decay_rate):
    first_new = beta_one * moment_one + (1.0 - beta_one) * grad_sum
    second_new = beta_two * moment_two + (1.0 - beta_two) * grad_sum * grad_sum
    first_hat = first_new / (1.0 - beta_one ** adam_step)
    second_hat = second_new / (1.0 - beta_two ** adam_step)
    updated = weight - step_rate * (first_hat / (jnp.sqrt(second_hat) + adam_eps) + decay_rate * weight)
    return (updated, first_new, second_new)

def reference(block_in, out_grad, norm_gain, in_proj, bc_proj, dt_proj, out_proj, chan_params, head_params, bc_conv, first_norm_gain, second_norm_gain, first_in_proj, second_in_proj, first_bc_proj, second_bc_proj, first_dt_proj, second_dt_proj, first_out_proj, second_out_proj, first_chan_params, second_chan_params, first_head_params, second_head_params, first_bc_conv, second_bc_conv):
    weights_b = (in_proj.astype(jnp.bfloat16), bc_proj.astype(jnp.bfloat16), dt_proj.astype(jnp.bfloat16), out_proj.astype(jnp.bfloat16))
    small_params = (norm_gain, chan_params, head_params, bc_conv)
    params = (norm_gain, in_proj, bc_proj, dt_proj, out_proj, chan_params, head_params, bc_conv)
    grads_zero = tuple((jnp.zeros(source.shape, jnp.float32) for source in params))

    def per_sequence(carry_grads, pair):
        out_rows, in_rows, grads = one_sequence(pair[0], pair[1], weights_b, small_params)
        return (jax.tree.map(jnp.add, carry_grads, grads), (out_rows, in_rows))
    grads_all, stacked = lax.scan(per_sequence, grads_zero, (block_in, out_grad))
    block_out, in_grad = stacked
    g_gain, g_zx, g_bc, g_dt, g_out, g_chan, g_head, g_bcconv = grads_all
    new_gain, nf_gain, ns_gain = adamw(norm_gain, g_gain, first_norm_gain, second_norm_gain, rate_vector, 0.0)
    new_zx, nf_zx, ns_zx = adamw(in_proj, g_zx, first_in_proj, second_in_proj, rate_matrix, decay_matrix)
    new_bc, nf_bc, ns_bc = adamw(bc_proj, g_bc, first_bc_proj, second_bc_proj, rate_matrix, decay_matrix)
    new_dt, nf_dt, ns_dt = adamw(dt_proj, g_dt, first_dt_proj, second_dt_proj, rate_matrix, decay_matrix)
    new_out, nf_out, ns_out = adamw(out_proj, g_out, first_out_proj, second_out_proj, rate_matrix, decay_matrix)
    new_chan, nf_chan, ns_chan = adamw(chan_params, g_chan, first_chan_params, second_chan_params, rate_vector, 0.0)
    new_head, nf_head, ns_head = adamw(head_params, g_head, first_head_params, second_head_params, rate_vector, 0.0)
    new_bcconv, nf_bcconv, ns_bcconv = adamw(bc_conv, g_bcconv, first_bc_conv, second_bc_conv, rate_vector, 0.0)
    return (block_out, in_grad, g_gain, g_zx, g_bc, g_dt, g_out, g_chan, g_head, g_bcconv, new_gain, new_zx, new_bc, new_dt, new_out, new_chan, new_head, new_bcconv, nf_gain, ns_gain, nf_zx, ns_zx, nf_bc, ns_bc, nf_dt, ns_dt, nf_out, ns_out, nf_chan, ns_chan, nf_head, ns_head, nf_bcconv, ns_bcconv)
```

```python
import jax
import jax.numpy as jnp
from jax import lax
from jax.experimental import pallas as pl
from jax.experimental.pallas import tpu as pltpu
from jax.sharding import PartitionSpec as P

D = 768
P_SIZE = 64
N = 128
K = 4
Q = 256
DI = 1536


eps_norm = 1e-05
beta_one = 0.9
beta_two = 0.95
adam_eps = 1e-08
rate_matrix = 0.01
rate_vector = 0.1
decay_matrix = 0.1
adam_step = 3.0
highest = lax.Precision.HIGHEST


def shifted(value, axis, steps):
    count = lax.axis_size(axis)
    leading, last = (max(0, -steps), min(count, count - steps))
    return lax.ppermute(value, axis, [(source, source + steps) for source in range(leading, last)])


def prefix(part, axis, combine, identity, reverse):
    count = lax.axis_size(axis)
    place = lax.axis_index(axis)
    ahead = count - 1 - place if reverse else place
    gathered = jax.tree.map(lambda a: lax.all_gather(a, axis), part)
    state = jax.tree.map(lambda a, e: jnp.zeros_like(a) + jnp.asarray(e, a.dtype), part, identity)

    def one(lap, state):
        source = count - 1 - lap if reverse else lap
        return combine(
            state, jax.tree.map(lambda a: lax.dynamic_index_in_dim(a, source, 0, False), gathered)
        )

    return lax.fori_loop(0, ahead, one, state)


def silu_grad(values):
    sigmoid_v = jax.nn.sigmoid(values)
    return sigmoid_v * (1.0 + values * (1.0 - sigmoid_v))


def dot_first(left_op, right_op):
    return lax.dot_general(
        left_op, right_op, (((0,), (0,)), ((), ())), preferred_element_type=jnp.float32
    )


def dot_last(left_op, right_op):
    return lax.dot_general(
        left_op, right_op, (((1,), (1,)), ((), ())), preferred_element_type=jnp.float32
    )


def dot_plain(left_op, right_op, contract):
    return lax.dot_general(
        left_op, right_op, ((contract[:1], contract[1:]), ((), ())),
        precision=highest, preferred_element_type=jnp.float32,
    )


def row_spans(tokens):
    size = Q if tokens % Q == 0 else tokens
    return [(start, size) for start in range(0, tokens, size)]


def causal_decay(cum_col, cum_row, start):
    shape = (cum_col.shape[0], cum_row.shape[1])
    rows = lax.broadcasted_iota(jnp.int32, shape, 0) + start
    cols = lax.broadcasted_iota(jnp.int32, shape, 1)
    return jnp.exp(jnp.where(rows >= cols, cum_col - cum_row, -jnp.inf))


def half_select(values, lane):
    return jnp.where(lane < P_SIZE, values[:, 0:1], values[:, 1:2])


def forward_kernel(x_ref, b_ref, c_ref, cols_ref, rows_ref, y_ref, state_ref, scores):
    tokens = x_ref.shape[0]
    spans = row_spans(tokens)

    @pl.when(pl.program_id(0) == 0)
    def _():
        for start, size in spans:
            scores[start : start + size, :] = dot_plain(
                c_ref[start : start + size, :], b_ref[...], (1, 1)
            )

    cols = cols_ref[0]
    rows = rows_ref[0]
    for start, size in spans:
        width = start + size
        lane = lax.broadcasted_iota(jnp.int32, (size, x_ref.shape[1]), 1)
        outs = []
        for head in range(2):
            decay = causal_decay(
                cols[start:width, head : head + 1], rows[head : head + 1, :width], start
            )
            mixing = scores[start:width, :width] * decay * rows[2 + head : 3 + head, :width]
            outs.append(dot_plain(mixing, x_ref[:width, :], (1, 0)))
        y_ref[start:width, :] = jnp.where(lane < P_SIZE, outs[0], outs[1])
    lane = lax.broadcasted_iota(jnp.int32, x_ref.shape, 1)
    weight = jnp.exp(cols[tokens - 1 :, :2] - cols[:, :2]) * cols[:, 2:]
    state_ref[...] = dot_plain(x_ref[...] * half_select(weight, lane), b_ref[...], (0, 0))


def backward_kernel(
    x_ref, b_ref, c_ref, cols_ref, rows_ref, dy_ref, state_ref, dstate_ref,
    dx_ref, db_ref, dc_ref, dcols_ref, drows_ref, scores, dscores, dx_acc,
):
    tokens = x_ref.shape[0]
    spans = row_spans(tokens)
    last = pl.program_id(0) == pl.num_programs(0) - 1

    @pl.when(pl.program_id(0) == 0)
    def _():
        for start, size in spans:
            scores[start : start + size, :] = dot_plain(
                c_ref[start : start + size, :], b_ref[...], (1, 1)
            )
        dscores[...] = jnp.zeros_like(dscores)
        db_ref[...] = jnp.zeros_like(db_ref)
        dc_ref[...] = jnp.zeros_like(dc_ref)

    cols = cols_ref[0]
    rows = rows_ref[0]
    lane = lax.broadcasted_iota(jnp.int32, x_ref.shape, 1)
    grow = jnp.exp(cols[:, :2])
    rest = jnp.exp(cols[tokens - 1 :, :2] - cols[:, :2])
    weight = rest * cols[:, 2:]
    x_all = x_ref[...]
    dy_all = dy_ref[...]
    weight_lane = half_select(weight, lane)
    dc_ref[...] += dot_plain(dy_all * half_select(grow, lane), state_ref[...], (1, 0))
    db_ref[...] += dot_plain(x_all * weight_lane, dstate_ref[...], (1, 0))
    from_state = dy_all * dot_plain(c_ref[...], state_ref[...], (1, 1))
    from_end = dot_plain(b_ref[...], dstate_ref[...], (1, 1))
    dx_acc[...] = from_end * weight_lane
    to_end = x_all * from_end
    pair_state = dstate_ref[...] * state_ref[...]
    last_row = lax.broadcasted_iota(jnp.int32, (tokens, 1), 0) == tokens - 1
    for head in range(2):
        mine = (lane < P_SIZE) if head == 0 else (lane >= P_SIZE)
        in_sum = jnp.sum(jnp.where(mine, from_state, 0.0), axis=1, keepdims=True)
        end_sum = jnp.sum(jnp.where(mine, to_end, 0.0), axis=1, keepdims=True)
        spent = weight[:, head : head + 1] * end_sum
        half = pair_state[head * P_SIZE : (head + 1) * P_SIZE, :]
        total = jnp.sum(spent, keepdims=True) + grow[tokens - 1 :, head : head + 1] * jnp.sum(
            half, keepdims=True
        )
        dcum = grow[:, head : head + 1] * in_sum - spent + jnp.where(last_row, total, 0.0)
        dcols_ref[0, :, head : head + 1] = dcum
        dcols_ref[0, :, 2 + head : 3 + head] = rest[:, head : head + 1] * end_sum
        dy_mine = jnp.where(mine, dy_all, 0.0)
        drows_ref[0, head : head + 1, :] = jnp.zeros((1, tokens), jnp.float32)
        for start, size in spans:
            width = start + size
            dt_row = rows[2 + head : 3 + head, :width]
            decay = causal_decay(
                cols[start:width, head : head + 1], rows[head : head + 1, :width], start
            )
            weighted = decay * dt_row
            dmix = dot_plain(dy_mine[start:width, :], x_all[:width, :], (1, 1))
            dscores[start:width, :width] += dmix * weighted
            mixing = scores[start:width, :width] * weighted
            dx_acc[:width, :] += dot_plain(mixing, dy_mine[start:width, :], (0, 0))
            dcols_ref[0, start:width, head : head + 1] += jnp.sum(
                dmix * mixing, axis=1, keepdims=True
            )
            drows_ref[0, head : head + 1, :width] += jnp.sum(
                dmix * decay * scores[start:width, :width], axis=0, keepdims=True
            )
    dx_ref[...] = dx_acc[...]

    @pl.when(last)
    def _():
        for start, size in spans:
            width = start + size
            dc_ref[start:width, :] += dot_plain(
                dscores[start:width, :width], b_ref[:width, :], (1, 0)
            )
            db_ref[:width, :] += dot_plain(
                dscores[start:width, :width], c_ref[start:width, :], (0, 0)
            )


def common_specs(tokens, pairs):
    wide = 2 * P_SIZE
    return [
        pl.BlockSpec((tokens, wide), lambda i: (0, i)),
        pl.BlockSpec((tokens, N), lambda i: (0, pairs)),
        pl.BlockSpec((tokens, N), lambda i: (0, pairs + 1)),
        pl.BlockSpec((1, tokens, 4), lambda i: (i, 0, 0)),
        pl.BlockSpec((1, 4, tokens), lambda i: (i, 0, 0)),
    ]


def ssd_forward(conv_all, cols, rows):
    tokens = conv_all.shape[0]
    pairs = cols.shape[0]
    wide = 2 * P_SIZE
    return pl.pallas_call(
        forward_kernel,
        grid=(pairs,),
        in_specs=common_specs(tokens, pairs),
        out_specs=[
            pl.BlockSpec((tokens, wide), lambda i: (0, i)),
            pl.BlockSpec((wide, N), lambda i: (i, 0)),
        ],
        out_shape=[
            jax.ShapeDtypeStruct((tokens, pairs * wide), jnp.float32),
            jax.ShapeDtypeStruct((pairs * wide, N), jnp.float32),
        ],
        scratch_shapes=[pltpu.VMEM((tokens, tokens), jnp.float32)],
        compiler_params=pltpu.CompilerParams(vmem_limit_bytes=32 << 20),
    )(conv_all, conv_all, conv_all, cols, rows)


def ssd_backward(conv_all, cols, rows, grad_ssd, state_in, grad_end):
    tokens = conv_all.shape[0]
    pairs = cols.shape[0]
    wide = 2 * P_SIZE
    pair_block = pl.BlockSpec((tokens, wide), lambda i: (0, i))
    state_block = pl.BlockSpec((wide, N), lambda i: (i, 0))
    shared_block = pl.BlockSpec((tokens, N), lambda i: (0, 0))
    return pl.pallas_call(
        backward_kernel,
        grid=(pairs,),
        in_specs=common_specs(tokens, pairs) + [pair_block, state_block, state_block],
        out_specs=[
            pair_block,
            shared_block,
            shared_block,
            pl.BlockSpec((1, tokens, 4), lambda i: (i, 0, 0)),
            pl.BlockSpec((1, 2, tokens), lambda i: (i, 0, 0)),
        ],
        out_shape=[
            jax.ShapeDtypeStruct((tokens, pairs * wide), jnp.float32),
            jax.ShapeDtypeStruct((tokens, N), jnp.float32),
            jax.ShapeDtypeStruct((tokens, N), jnp.float32),
            jax.ShapeDtypeStruct((pairs, tokens, 4), jnp.float32),
            jax.ShapeDtypeStruct((pairs, 2, tokens), jnp.float32),
        ],
        scratch_shapes=[
            pltpu.VMEM((tokens, tokens), jnp.float32),
            pltpu.VMEM((tokens, tokens), jnp.float32),
            pltpu.VMEM((tokens, wide), jnp.float32),
        ],
        compiler_params=pltpu.CompilerParams(vmem_limit_bytes=32 << 20),
    )(conv_all, conv_all, conv_all, cols, rows, grad_ssd, state_in, grad_end)


def combine_states(earlier, later):
    return (earlier[0] + later[0], jnp.exp(later[0])[:, None] * earlier[1] + later[1])


def adamw(weight, grad_sum, moment_one, moment_two, step_rate, decay_rate):
    first_new = beta_one * moment_one + (1.0 - beta_one) * grad_sum
    second_new = beta_two * moment_two + (1.0 - beta_two) * grad_sum * grad_sum
    first_hat = first_new / (1.0 - beta_one**adam_step)
    second_hat = second_new / (1.0 - beta_two**adam_step)
    updated = weight - step_rate * (
        first_hat / (jnp.sqrt(second_hat) + adam_eps) + decay_rate * weight
    )
    return (updated, first_new, second_new)


def per_device(
    block_in,
    out_grad,
    norm_gain,
    in_proj,
    bc_proj,
    dt_proj,
    out_proj,
    chan_params,
    head_params,
    bc_conv,
    first_norm_gain,
    second_norm_gain,
    first_in_proj,
    second_in_proj,
    first_bc_proj,
    second_bc_proj,
    first_dt_proj,
    second_dt_proj,
    first_out_proj,
    second_out_proj,
    first_chan_params,
    second_chan_params,
    first_head_params,
    second_head_params,
    first_bc_conv,
    second_bc_conv,
):
    shards = ("seq", "batch")
    block_rows = block_in[0]
    grad_rows = out_grad[0]
    tokens = block_rows.shape[0]
    head_local = head_params.shape[1]
    inner_local = chan_params.shape[1]
    shard_rows = in_proj.shape[1]
    pairs = head_local // 2
    edge_rows = K - 1
    half = jnp.bfloat16
    bc_heads = lax.all_gather(bc_proj.astype(half), "head", axis=0, tiled=True)
    spare = -head_local % 128
    packed = jnp.concatenate(
        [
            in_proj[0].astype(half),
            in_proj[1].astype(half),
            out_proj.astype(half).T,
            jnp.pad(dt_proj.astype(half), ((0, 0), (0, spare))),
            bc_heads.T.reshape(shard_rows, 2 * N),
        ],
        1,
    )
    full = lax.all_gather(packed, shards, axis=0, tiled=True)
    zx_full = full[:, : 2 * inner_local]
    out_t = full[:, 2 * inner_local : 3 * inner_local]
    dt_full = full[:, 3 * inner_local : 3 * inner_local + head_local]
    bc_t = full[:, 3 * inner_local + head_local + spare :].reshape(2 * N, D)
    block_f = block_rows.astype(jnp.float32)
    scaling_in = lax.rsqrt(jnp.mean(block_f * block_f, axis=-1, keepdims=True) + eps_norm)
    normed_b = (block_f * scaling_in * norm_gain[None, :]).astype(half)
    both_pre = jnp.dot(normed_b, zx_full, preferred_element_type=jnp.float32)
    gate_pre = both_pre[:, :inner_local]
    step_raw = jnp.dot(normed_b, dt_full, preferred_element_type=jnp.float32)
    conv_pre = jnp.concatenate([both_pre[:, inner_local:], dot_last(normed_b, bc_t)], 1)
    edge_in = shifted(conv_pre[tokens - edge_rows :], "seq", 1)
    padded = jnp.concatenate([edge_in, conv_pre], 0)
    taps = jnp.concatenate([chan_params[: K + 1], bc_conv], 1)
    summed = taps[K][None, :] + sum(
        taps[k][None, :] * padded[k : k + tokens] for k in range(K)
    )
    conv_all = jax.nn.silu(summed)
    inner_x = conv_all[:, :inner_local]
    c_rows = conv_all[:, inner_local + N :]
    steps_dt = jax.nn.softplus(step_raw + head_params[0][None, :])
    steps_log = -jnp.exp(head_params[1])[None, :] * steps_dt
    order = jnp.arange(tokens)
    lower = (order[:, None] >= order[None, :]).astype(jnp.float32)
    cumulative = jnp.dot(lower, steps_log, precision=highest)
    spread = (
        jnp.arange(head_local)[:, None] == jnp.arange(inner_local)[None, :] // P_SIZE
    ).astype(jnp.float32)
    decay_lane = jnp.dot(jnp.exp(cumulative), spread, precision=highest)
    rows = jnp.concatenate(
        [cumulative.T.reshape(pairs, 2, tokens), steps_dt.T.reshape(pairs, 2, tokens)], 1
    )
    cols = rows.transpose(0, 2, 1)
    local_out, local_state = ssd_forward(conv_all, cols, rows)
    device_log = jnp.repeat(cumulative[-1], P_SIZE)
    zero_log = jnp.zeros(device_log.shape, jnp.float32)
    zero_state = jnp.zeros(local_state.shape, jnp.float32)
    state_in = prefix(
        (device_log, local_state), "seq", combine_states, (zero_log, zero_state), False
    )[1]
    ssd_out = local_out + decay_lane * lax.dot_general(
        c_rows, state_in, (((1,), (1,)), ((), ())), precision=highest
    )
    skip_lane = jnp.repeat(head_params[2], P_SIZE)[None, :]
    mixed_rows = ssd_out + skip_lane * inner_x
    gate_act = jax.nn.silu(gate_pre)
    gated_rows = mixed_rows * gate_act
    gate_gain = chan_params[K + 1]
    grad_mixed = jnp.dot(grad_rows, out_t, preferred_element_type=jnp.float32)
    gain_grad = grad_mixed * gate_gain[None, :]
    square_sum, cross_sum = lax.psum(
        jnp.stack([jnp.sum(gated_rows * gated_rows, -1), jnp.sum(gain_grad * gated_rows, -1)]),
        "head",
    )
    scaling_gate = lax.rsqrt(square_sum / DI + eps_norm)[:, None]
    mixed_b = (gated_rows * scaling_gate * gate_gain[None, :]).astype(half)
    out_partial = dot_last(mixed_b, out_t)
    out_sum = lax.psum(out_partial.astype(half), "head")
    g_out_t = lax.psum_scatter(
        dot_first(grad_rows, mixed_b), shards, scatter_dimension=0, tiled=True
    )
    grad_f = grad_rows.astype(jnp.float32)
    grad_gate_gain = jnp.sum(grad_mixed * gated_rows * scaling_gate, axis=0)
    grad_gated = scaling_gate * gain_grad - gated_rows * scaling_gate**3 * cross_sum[:, None] / DI
    grad_gate_b = (grad_gated * mixed_rows * silu_grad(gate_pre)).astype(half)
    grad_ssd = grad_gated * gate_act
    grad_skip = jnp.sum(jnp.sum(grad_ssd * inner_x, axis=0).reshape(head_local, P_SIZE), -1)
    grad_direct = lax.dot_general(
        grad_ssd * decay_lane, c_rows, (((0,), (0,)), ((), ())), precision=highest
    )
    grad_end = prefix(
        (device_log, grad_direct), "seq", combine_states, (zero_log, zero_state), True
    )[1]
    grad_x, grad_b, grad_c, grad_cols, grad_rows_dt = ssd_backward(
        conv_all, cols, rows, grad_ssd, state_in, grad_end
    )
    grad_x, out_sum = lax.optimization_barrier((grad_x, out_sum))
    block_out = (block_f + out_sum.astype(jnp.float32)).astype(half)

    def per_head(values):
        return values.transpose(0, 2, 1).reshape(head_local, tokens)

    row_dt = grad_rows_dt.reshape(head_local, tokens)
    grad_dt_t = row_dt + per_head(grad_cols[:, :, 2:])
    steps_dt_t = rows[:, 2:].reshape(head_local, tokens)
    grad_cum_t = per_head(grad_cols[:, :, :2]) - row_dt * steps_dt_t
    grad_log_t = jnp.dot(grad_cum_t, lower, precision=highest)
    decay_rate = jnp.exp(head_params[1])[:, None]
    sigmoid_t = 1.0 - jnp.exp(-steps_dt_t)
    grad_step_t = (grad_dt_t - decay_rate * grad_log_t) * sigmoid_t
    grad_log_rate = -jnp.sum(grad_log_t * decay_rate * steps_dt_t, axis=1)
    grad_head = jnp.stack([jnp.sum(grad_step_t, axis=1), grad_log_rate, grad_skip])
    grad_act = jnp.concatenate([grad_x + skip_lane * grad_ssd, grad_b, grad_c], 1)
    grad_pre = grad_act * silu_grad(summed)
    edge_back = shifted(grad_pre[:edge_rows], "seq", -1)
    grad_ext = jnp.concatenate([grad_pre, edge_back], 0)
    grad_conv_b = sum(
        taps[k][None, :] * grad_ext[edge_rows - k : edge_rows - k + tokens] for k in range(K)
    ).astype(half)
    grad_taps = jnp.stack(
        [jnp.sum(padded[k : k + tokens] * grad_pre, axis=0) for k in range(K)]
        + [jnp.sum(grad_pre, axis=0)]
    )
    grad_inner_b = grad_conv_b[:, :inner_local]
    grad_bc_b = grad_conv_b[:, inner_local:]
    grad_step_b = grad_step_t.T.astype(half)
    both_b = jnp.concatenate([grad_gate_b, grad_inner_b], 1)
    grad_normed = (
        dot_last(both_b, zx_full)
        + jnp.dot(grad_bc_b, bc_t, preferred_element_type=jnp.float32)
        + dot_last(grad_step_b, dt_full)
    )
    bc_partial = dot_first(grad_bc_b, normed_b)
    bcconv_rows = jnp.pad(grad_taps[:, inner_local:], ((0, -(K + 1) % 8), (0, D - 2 * N)))
    summed_heads = lax.psum(
        jnp.concatenate([grad_normed, bc_partial, bcconv_rows], 0).astype(half), "head"
    ).astype(jnp.float32)
    grad_normed = summed_heads[:tokens]
    row_block = D // lax.axis_size("head")
    bc_own = lax.dynamic_slice_in_dim(
        summed_heads[tokens : tokens + 2 * N], lax.axis_index("head") * row_block, row_block, 1
    )
    grad_in_cat = jnp.concatenate(
        [
            dot_first(normed_b, both_b),
            jnp.pad(dot_first(normed_b, grad_step_b), ((0, 0), (0, spare))),
        ],
        1,
    )
    g_in_cat = lax.psum_scatter(grad_in_cat, shards, scatter_dimension=0, tiled=True)
    g_bc = lax.psum_scatter(bc_own, shards, scatter_dimension=0, tiled=True).T
    scaled_grad = grad_normed * norm_gain[None, :]
    grad_norm_gain = jnp.sum(grad_normed * block_f * scaling_in, axis=0)
    in_rows = (
        grad_f
        + scaling_in * scaled_grad
        - block_f * scaling_in**3 * jnp.sum(scaled_grad * block_f, axis=-1, keepdims=True) / D
    )
    g_zx = jnp.stack([g_in_cat[:, :inner_local], g_in_cat[:, inner_local : 2 * inner_local]])
    g_dt = g_in_cat[:, 2 * inner_local : 2 * inner_local + head_local]
    g_out = g_out_t.T
    grad_chan = jnp.concatenate([grad_taps[:, :inner_local], grad_gate_gain[None, :]], 0)
    grad_bcconv = summed_heads[tokens + 2 * N : tokens + 2 * N + K + 1, : 2 * N]
    g_gain, g_chan, g_head, g_bcconv = lax.psum(
        (grad_norm_gain, grad_chan, grad_head, grad_bcconv), shards
    )
    new_gain, nf_gain, ns_gain = adamw(
        norm_gain, g_gain, first_norm_gain, second_norm_gain, rate_vector, 0.0
    )
    new_zx, nf_zx, ns_zx = adamw(
        in_proj, g_zx, first_in_proj, second_in_proj, rate_matrix, decay_matrix
    )
    new_bc, nf_bc, ns_bc = adamw(
        bc_proj, g_bc, first_bc_proj, second_bc_proj, rate_matrix, decay_matrix
    )
    new_dt, nf_dt, ns_dt = adamw(
        dt_proj, g_dt, first_dt_proj, second_dt_proj, rate_matrix, decay_matrix
    )
    new_out, nf_out, ns_out = adamw(
        out_proj, g_out, first_out_proj, second_out_proj, rate_matrix, decay_matrix
    )
    new_chan, nf_chan, ns_chan = adamw(
        chan_params, g_chan, first_chan_params, second_chan_params, rate_vector, 0.0
    )
    new_head, nf_head, ns_head = adamw(
        head_params, g_head, first_head_params, second_head_params, rate_vector, 0.0
    )
    new_bcconv, nf_bcconv, ns_bcconv = adamw(
        bc_conv, g_bcconv, first_bc_conv, second_bc_conv, rate_vector, 0.0
    )
    return (
        block_out[None],
        in_rows[None],
        g_gain,
        g_zx,
        g_bc,
        g_dt,
        g_out,
        g_chan,
        g_head,
        g_bcconv,
        new_gain,
        new_zx,
        new_bc,
        new_dt,
        new_out,
        new_chan,
        new_head,
        new_bcconv,
        nf_gain,
        ns_gain,
        nf_zx,
        ns_zx,
        nf_bc,
        ns_bc,
        nf_dt,
        ns_dt,
        nf_out,
        ns_out,
        nf_chan,
        ns_chan,
        nf_head,
        ns_head,
        nf_bcconv,
        ns_bcconv,
    )


def solution(mesh):
    in_specs = (
        P("batch", "seq", None),
        P("batch", "seq", None),
        P(),
        P(None, ("seq", "batch"), "head"),
        P("head", ("seq", "batch")),
        P(("seq", "batch"), "head"),
        P("head", ("seq", "batch")),
        P(None, "head"),
        P(None, "head"),
        P(),
        P(),
        P(),
        P(None, ("seq", "batch"), "head"),
        P(None, ("seq", "batch"), "head"),
        P("head", ("seq", "batch")),
        P("head", ("seq", "batch")),
        P(("seq", "batch"), "head"),
        P(("seq", "batch"), "head"),
        P("head", ("seq", "batch")),
        P("head", ("seq", "batch")),
        P(None, "head"),
        P(None, "head"),
        P(None, "head"),
        P(None, "head"),
        P(),
        P(),
    )
    out_specs = (
        P("batch", "seq", None),
        P("batch", "seq", None),
        P(),
        P(None, ("seq", "batch"), "head"),
        P("head", ("seq", "batch")),
        P(("seq", "batch"), "head"),
        P("head", ("seq", "batch")),
        P(None, "head"),
        P(None, "head"),
        P(),
        P(),
        P(None, ("seq", "batch"), "head"),
        P("head", ("seq", "batch")),
        P(("seq", "batch"), "head"),
        P("head", ("seq", "batch")),
        P(None, "head"),
        P(None, "head"),
        P(),
        P(),
        P(),
        P(None, ("seq", "batch"), "head"),
        P(None, ("seq", "batch"), "head"),
        P("head", ("seq", "batch")),
        P("head", ("seq", "batch")),
        P(("seq", "batch"), "head"),
        P(("seq", "batch"), "head"),
        P("head", ("seq", "batch")),
        P("head", ("seq", "batch")),
        P(None, "head"),
        P(None, "head"),
        P(None, "head"),
        P(None, "head"),
        P(),
        P(),
    )
    return jax.shard_map(
        per_device, mesh=mesh, in_specs=in_specs, out_specs=out_specs, check_vma=False
    )
```

```python
import functools

import jax
import jax.numpy as jnp
from jax import lax
from jax.experimental import pallas as pl
from jax.experimental.pallas import tpu as pltpu
from jax.sharding import PartitionSpec as P

D = 768
P_SIZE = 64
N = 128
K = 4
Q = 256
DI = 1536


eps_norm = 1e-05
beta_one = 0.9
beta_two = 0.95
adam_eps = 1e-08
rate_matrix = 0.01
rate_vector = 0.1
decay_matrix = 0.1
adam_step = 3.0
highest = lax.Precision.HIGHEST


def shifted(value, axis, steps):
    count = lax.axis_size(axis)
    leading, last = (max(0, -steps), min(count, count - steps))
    return lax.ppermute(value, axis, [(source, source + steps) for source in range(leading, last)])


def prefix(part, axis, combine, identity, reverse):
    count = lax.axis_size(axis)
    place = lax.axis_index(axis)
    ahead = count - 1 - place if reverse else place
    gathered = jax.tree.map(lambda a: lax.all_gather(a, axis), part)
    state = jax.tree.map(lambda a, e: jnp.zeros_like(a) + jnp.asarray(e, a.dtype), part, identity)

    def one(lap, state):
        source = count - 1 - lap if reverse else lap
        return combine(
            state, jax.tree.map(lambda a: lax.dynamic_index_in_dim(a, source, 0, False), gathered)
        )

    return lax.fori_loop(0, ahead, one, state)


def silu_grad(values):
    sigmoid_v = jax.nn.sigmoid(values)
    return sigmoid_v * (1.0 + values * (1.0 - sigmoid_v))


def dot_first(left_op, right_op):
    return lax.dot_general(
        left_op, right_op, (((0,), (0,)), ((), ())), preferred_element_type=jnp.float32
    )


def dot_last(left_op, right_op):
    return lax.dot_general(
        left_op, right_op, (((1,), (1,)), ((), ())), preferred_element_type=jnp.float32
    )


def dot_plain(left_op, right_op, contract):
    return lax.dot_general(
        left_op, right_op, ((contract[:1], contract[1:]), ((), ())),
        precision=highest, preferred_element_type=jnp.float32,
    )


def row_spans(tokens):
    size = Q if tokens % Q == 0 else tokens
    return [(start, size) for start in range(0, tokens, size)]


def causal_decay(cum_col, cum_row, start):
    shape = (cum_col.shape[0], cum_row.shape[1])
    rows = lax.broadcasted_iota(jnp.int32, shape, 0) + start
    cols = lax.broadcasted_iota(jnp.int32, shape, 1)
    return jnp.exp(jnp.where(rows >= cols, cum_col - cum_row, -jnp.inf))


def half_select(values, lane):
    return jnp.where(lane < P_SIZE, values[:, 0:1], values[:, 1:2])


def forward_kernel(x_ref, b_ref, c_ref, cols_ref, rows_ref, y_ref, state_ref, scores):
    tokens = x_ref.shape[0]
    spans = row_spans(tokens)

    @pl.when(pl.program_id(0) == 0)
    def _():
        for start, size in spans:
            scores[start : start + size, :] = dot_plain(
                c_ref[start : start + size, :], b_ref[...], (1, 1)
            )

    cols = cols_ref[0]
    rows = rows_ref[0]
    for start, size in spans:
        width = start + size
        lane = lax.broadcasted_iota(jnp.int32, (size, x_ref.shape[1]), 1)
        outs = []
        for head in range(2):
            decay = causal_decay(
                cols[start:width, head : head + 1], rows[head : head + 1, :width], start
            )
            mixing = scores[start:width, :width] * decay * rows[2 + head : 3 + head, :width]
            outs.append(dot_plain(mixing, x_ref[:width, :], (1, 0)))
        y_ref[start:width, :] = jnp.where(lane < P_SIZE, outs[0], outs[1])
    lane = lax.broadcasted_iota(jnp.int32, x_ref.shape, 1)
    weight = jnp.exp(cols[tokens - 1 :, :2] - cols[:, :2]) * cols[:, 2:]
    state_ref[...] = dot_plain(x_ref[...] * half_select(weight, lane), b_ref[...], (0, 0))


def backward_kernel(
    x_ref, b_ref, c_ref, cols_ref, rows_ref, dy_ref, state_ref, dstate_ref,
    dx_ref, db_ref, dc_ref, dcols_ref, drows_ref, scores, dscores, dx_acc,
):
    tokens = x_ref.shape[0]
    spans = row_spans(tokens)
    last = pl.program_id(0) == pl.num_programs(0) - 1

    @pl.when(pl.program_id(0) == 0)
    def _():
        for start, size in spans:
            scores[start : start + size, :] = dot_plain(
                c_ref[start : start + size, :], b_ref[...], (1, 1)
            )
        dscores[...] = jnp.zeros_like(dscores)
        db_ref[...] = jnp.zeros_like(db_ref)
        dc_ref[...] = jnp.zeros_like(dc_ref)

    cols = cols_ref[0]
    rows = rows_ref[0]
    lane = lax.broadcasted_iota(jnp.int32, x_ref.shape, 1)
    grow = jnp.exp(cols[:, :2])
    rest = jnp.exp(cols[tokens - 1 :, :2] - cols[:, :2])
    weight = rest * cols[:, 2:]
    x_all = x_ref[...]
    dy_all = dy_ref[...]
    weight_lane = half_select(weight, lane)
    dc_ref[...] += dot_plain(dy_all * half_select(grow, lane), state_ref[...], (1, 0))
    db_ref[...] += dot_plain(x_all * weight_lane, dstate_ref[...], (1, 0))
    from_state = dy_all * dot_plain(c_ref[...], state_ref[...], (1, 1))
    from_end = dot_plain(b_ref[...], dstate_ref[...], (1, 1))
    dx_acc[...] = from_end * weight_lane
    to_end = x_all * from_end
    pair_state = dstate_ref[...] * state_ref[...]
    last_row = lax.broadcasted_iota(jnp.int32, (tokens, 1), 0) == tokens - 1
    for head in range(2):
        mine = (lane < P_SIZE) if head == 0 else (lane >= P_SIZE)
        in_sum = jnp.sum(jnp.where(mine, from_state, 0.0), axis=1, keepdims=True)
        end_sum = jnp.sum(jnp.where(mine, to_end, 0.0), axis=1, keepdims=True)
        spent = weight[:, head : head + 1] * end_sum
        half = pair_state[head * P_SIZE : (head + 1) * P_SIZE, :]
        total = jnp.sum(spent, keepdims=True) + grow[tokens - 1 :, head : head + 1] * jnp.sum(
            half, keepdims=True
        )
        dcum = grow[:, head : head + 1] * in_sum - spent + jnp.where(last_row, total, 0.0)
        dcols_ref[0, :, head : head + 1] = dcum
        dcols_ref[0, :, 2 + head : 3 + head] = rest[:, head : head + 1] * end_sum
        dy_mine = jnp.where(mine, dy_all, 0.0)
        drows_ref[0, head : head + 1, :] = jnp.zeros((1, tokens), jnp.float32)
        for start, size in spans:
            width = start + size
            dt_row = rows[2 + head : 3 + head, :width]
            decay = causal_decay(
                cols[start:width, head : head + 1], rows[head : head + 1, :width], start
            )
            weighted = decay * dt_row
            dmix = dot_plain(dy_mine[start:width, :], x_all[:width, :], (1, 1))
            dscores[start:width, :width] += dmix * weighted
            mixing = scores[start:width, :width] * weighted
            dx_acc[:width, :] += dot_plain(mixing, dy_mine[start:width, :], (0, 0))
            dcols_ref[0, start:width, head : head + 1] += jnp.sum(
                dmix * mixing, axis=1, keepdims=True
            )
            drows_ref[0, head : head + 1, :width] += jnp.sum(
                dmix * decay * scores[start:width, :width], axis=0, keepdims=True
            )
    dx_ref[...] = dx_acc[...]

    @pl.when(last)
    def _():
        for start, size in spans:
            width = start + size
            dc_ref[start:width, :] += dot_plain(
                dscores[start:width, :width], b_ref[:width, :], (1, 0)
            )
            db_ref[:width, :] += dot_plain(
                dscores[start:width, :width], c_ref[start:width, :], (0, 0)
            )


def common_specs(tokens, pairs):
    wide = 2 * P_SIZE
    return [
        pl.BlockSpec((tokens, wide), lambda i: (0, i)),
        pl.BlockSpec((tokens, N), lambda i: (0, pairs)),
        pl.BlockSpec((tokens, N), lambda i: (0, pairs + 1)),
        pl.BlockSpec((1, tokens, 4), lambda i: (i, 0, 0)),
        pl.BlockSpec((1, 4, tokens), lambda i: (i, 0, 0)),
    ]


def ssd_forward(conv_all, cols, rows):
    tokens = conv_all.shape[0]
    pairs = cols.shape[0]
    wide = 2 * P_SIZE
    return pl.pallas_call(
        forward_kernel,
        grid=(pairs,),
        in_specs=common_specs(tokens, pairs),
        out_specs=[
            pl.BlockSpec((tokens, wide), lambda i: (0, i)),
            pl.BlockSpec((wide, N), lambda i: (i, 0)),
        ],
        out_shape=[
            jax.ShapeDtypeStruct((tokens, pairs * wide), jnp.float32),
            jax.ShapeDtypeStruct((pairs * wide, N), jnp.float32),
        ],
        scratch_shapes=[pltpu.VMEM((tokens, tokens), jnp.float32)],
        compiler_params=pltpu.CompilerParams(vmem_limit_bytes=32 << 20),
    )(conv_all, conv_all, conv_all, cols, rows)


def ssd_backward(conv_all, cols, rows, grad_ssd, state_in, grad_end):
    tokens = conv_all.shape[0]
    pairs = cols.shape[0]
    wide = 2 * P_SIZE
    pair_block = pl.BlockSpec((tokens, wide), lambda i: (0, i))
    state_block = pl.BlockSpec((wide, N), lambda i: (i, 0))
    shared_block = pl.BlockSpec((tokens, N), lambda i: (0, 0))
    return pl.pallas_call(
        backward_kernel,
        grid=(pairs,),
        in_specs=common_specs(tokens, pairs) + [pair_block, state_block, state_block],
        out_specs=[
            pair_block,
            shared_block,
            shared_block,
            pl.BlockSpec((1, tokens, 4), lambda i: (i, 0, 0)),
            pl.BlockSpec((1, 2, tokens), lambda i: (i, 0, 0)),
        ],
        out_shape=[
            jax.ShapeDtypeStruct((tokens, pairs * wide), jnp.float32),
            jax.ShapeDtypeStruct((tokens, N), jnp.float32),
            jax.ShapeDtypeStruct((tokens, N), jnp.float32),
            jax.ShapeDtypeStruct((pairs, tokens, 4), jnp.float32),
            jax.ShapeDtypeStruct((pairs, 2, tokens), jnp.float32),
        ],
        scratch_shapes=[
            pltpu.VMEM((tokens, tokens), jnp.float32),
            pltpu.VMEM((tokens, tokens), jnp.float32),
            pltpu.VMEM((tokens, wide), jnp.float32),
        ],
        compiler_params=pltpu.CompilerParams(vmem_limit_bytes=32 << 20),
    )(conv_all, conv_all, conv_all, cols, rows, grad_ssd, state_in, grad_end)


def greet(peers):
    barrier = pltpu.get_barrier_semaphore()
    for peer in peers:
        pl.semaphore_signal(
            barrier, inc=1, device_id=peer, device_id_type=pl.DeviceIdType.MESH
        )
    pl.semaphore_wait(barrier, len(peers))


def head_sum_kernel(count, x_ref, out_ref, slots, total, send_one, recv_one, send_two, recv_two):
    me = lax.axis_index("head")
    rows = x_ref.shape[0] // count
    peers = [lax.rem(me + lap, count) for lap in range(1, count)]
    greet([{"head": peer} for peer in peers])

    def span(place):
        return pl.ds(pl.multiple_of(place * rows, 16), rows)

    first = [
        pltpu.make_async_remote_copy(
            src_ref=x_ref.at[span(peer)],
            dst_ref=slots.at[lap],
            send_sem=send_one.at[lap],
            recv_sem=recv_one.at[lap],
            device_id={"head": peer},
            device_id_type=pl.DeviceIdType.MESH,
        )
        for lap, peer in enumerate(peers)
    ]
    for copy in first:
        copy.start()
    acc = x_ref[span(me), :].astype(jnp.float32)
    for lap, copy in enumerate(first):
        copy.wait()
        acc = acc + slots[lap].astype(jnp.float32)
    total[...] = acc.astype(total.dtype)
    out_ref[span(me), :] = total[...]
    second = [
        pltpu.make_async_remote_copy(
            src_ref=total,
            dst_ref=out_ref.at[span(me)],
            send_sem=send_two.at[lap],
            recv_sem=recv_two.at[lap],
            device_id={"head": peer},
            device_id_type=pl.DeviceIdType.MESH,
        )
        for lap, peer in enumerate(peers)
    ]
    for copy in second:
        copy.start()
    for copy in second:
        copy.wait()


def head_sum(values):
    count = lax.axis_size("head")
    if count == 1:
        return values
    rows, width = values.shape
    vmem = pl.BlockSpec(memory_space=pltpu.VMEM)
    sems = pltpu.SemaphoreType.DMA((count - 1,))
    return pl.pallas_call(
        functools.partial(head_sum_kernel, count),
        out_shape=jax.ShapeDtypeStruct(values.shape, values.dtype),
        in_specs=[vmem],
        out_specs=vmem,
        scratch_shapes=[
            pltpu.VMEM((count - 1, rows // count, width), values.dtype),
            pltpu.VMEM((rows // count, width), values.dtype),
            sems,
            sems,
            sems,
            sems,
        ],
        compiler_params=pltpu.CompilerParams(
            collective_id=0, has_side_effects=True, vmem_limit_bytes=16 << 20
        ),
    )(values)


def shard_sum_kernel(
    counts, small_ref, part_ref, small_out, part_out,
    small_slots, part_slots, send_one, recv_one, send_two, recv_two,
):
    seqs, batches = counts
    count = seqs * batches
    me = lax.axis_index("seq") * batches + lax.axis_index("batch")
    places = [lax.rem(me + lap, count) for lap in range(1, count)]
    peers = [
        {"seq": lax.div(place, batches), "batch": lax.rem(place, batches)} for place in places
    ]
    greet(peers)
    copies = []
    for lap, (place, peer) in enumerate(zip(places, peers)):
        for source, slots, send, recv in (
            (small_ref, small_slots, send_one, recv_one),
            (part_ref.at[place], part_slots, send_two, recv_two),
        ):
            copies.append(
                pltpu.make_async_remote_copy(
                    src_ref=source,
                    dst_ref=slots.at[me],
                    send_sem=send.at[lap],
                    recv_sem=recv.at[lap],
                    device_id=peer,
                    device_id_type=pl.DeviceIdType.MESH,
                )
            )
    for copy in copies:
        copy.start()
    small_slots[me] = small_ref[...]
    part_slots[me] = part_ref[me]
    for copy in copies:
        copy.wait()
    small_out[...] = sum(small_slots[place] for place in range(count))
    part_out[...] = sum(part_slots[place] for place in range(count))


def shard_sum(small, part):
    counts = (lax.axis_size("seq"), lax.axis_size("batch"))
    count = part.shape[0]
    if count == 1:
        return small, part[0]
    vmem = pl.BlockSpec(memory_space=pltpu.VMEM)
    sems = pltpu.SemaphoreType.DMA((count - 1,))
    return pl.pallas_call(
        functools.partial(shard_sum_kernel, counts),
        out_shape=[
            jax.ShapeDtypeStruct(small.shape, small.dtype),
            jax.ShapeDtypeStruct(part.shape[1:], part.dtype),
        ],
        in_specs=[vmem, vmem],
        out_specs=[vmem, vmem],
        scratch_shapes=[
            pltpu.VMEM((count,) + small.shape, small.dtype),
            pltpu.VMEM(part.shape, part.dtype),
            sems,
            sems,
            sems,
            sems,
        ],
        compiler_params=pltpu.CompilerParams(
            collective_id=1, has_side_effects=True, vmem_limit_bytes=16 << 20
        ),
    )(small, part)


def combine_states(earlier, later):
    return (earlier[0] + later[0], jnp.exp(later[0])[:, None] * earlier[1] + later[1])


def adamw(weight, grad_sum, moment_one, moment_two, step_rate, decay_rate):
    first_new = beta_one * moment_one + (1.0 - beta_one) * grad_sum
    second_new = beta_two * moment_two + (1.0 - beta_two) * grad_sum * grad_sum
    first_hat = first_new / (1.0 - beta_one**adam_step)
    second_hat = second_new / (1.0 - beta_two**adam_step)
    updated = weight - step_rate * (
        first_hat / (jnp.sqrt(second_hat) + adam_eps) + decay_rate * weight
    )
    return (updated, first_new, second_new)


def per_device(
    block_in,
    out_grad,
    norm_gain,
    in_proj,
    bc_proj,
    dt_proj,
    out_proj,
    chan_params,
    head_params,
    bc_conv,
    first_norm_gain,
    second_norm_gain,
    first_in_proj,
    second_in_proj,
    first_bc_proj,
    second_bc_proj,
    first_dt_proj,
    second_dt_proj,
    first_out_proj,
    second_out_proj,
    first_chan_params,
    second_chan_params,
    first_head_params,
    second_head_params,
    first_bc_conv,
    second_bc_conv,
):
    shards = ("seq", "batch")
    block_rows = block_in[0]
    grad_rows = out_grad[0]
    tokens = block_rows.shape[0]
    head_local = head_params.shape[1]
    inner_local = chan_params.shape[1]
    shard_rows = in_proj.shape[1]
    pairs = head_local // 2
    edge_rows = K - 1
    half = jnp.bfloat16
    bc_heads = lax.all_gather(bc_proj.astype(half), "head", axis=0, tiled=True)
    spare = -head_local % 128
    packed = jnp.concatenate(
        [
            in_proj[0].astype(half),
            in_proj[1].astype(half),
            out_proj.astype(half).T,
            jnp.pad(dt_proj.astype(half), ((0, 0), (0, spare))),
            bc_heads.T.reshape(shard_rows, 2 * N),
        ],
        1,
    )
    full = lax.all_gather(packed, shards, axis=0, tiled=True)
    zx_full = full[:, : 2 * inner_local]
    out_t = full[:, 2 * inner_local : 3 * inner_local]
    dt_full = full[:, 3 * inner_local : 3 * inner_local + head_local]
    bc_t = full[:, 3 * inner_local + head_local + spare :].reshape(2 * N, D)
    block_f = block_rows.astype(jnp.float32)
    scaling_in = lax.rsqrt(jnp.mean(block_f * block_f, axis=-1, keepdims=True) + eps_norm)
    normed_b = (block_f * scaling_in * norm_gain[None, :]).astype(half)
    both_pre = jnp.dot(normed_b, zx_full, preferred_element_type=jnp.float32)
    gate_pre = both_pre[:, :inner_local]
    step_raw = jnp.dot(normed_b, dt_full, preferred_element_type=jnp.float32)
    conv_pre = jnp.concatenate([both_pre[:, inner_local:], dot_last(normed_b, bc_t)], 1)
    edge_in = shifted(conv_pre[tokens - edge_rows :], "seq", 1)
    padded = jnp.concatenate([edge_in, conv_pre], 0)
    taps = jnp.concatenate([chan_params[: K + 1], bc_conv], 1)
    summed = taps[K][None, :] + sum(
        taps[k][None, :] * padded[k : k + tokens] for k in range(K)
    )
    conv_all = jax.nn.silu(summed)
    inner_x = conv_all[:, :inner_local]
    c_rows = conv_all[:, inner_local + N :]
    steps_dt = jax.nn.softplus(step_raw + head_params[0][None, :])
    steps_log = -jnp.exp(head_params[1])[None, :] * steps_dt
    order = jnp.arange(tokens)
    lower = (order[:, None] >= order[None, :]).astype(jnp.float32)
    cumulative = jnp.dot(lower, steps_log, precision=highest)
    spread = (
        jnp.arange(head_local)[:, None] == jnp.arange(inner_local)[None, :] // P_SIZE
    ).astype(jnp.float32)
    decay_lane = jnp.dot(jnp.exp(cumulative), spread, precision=highest)
    rows = jnp.concatenate(
        [cumulative.T.reshape(pairs, 2, tokens), steps_dt.T.reshape(pairs, 2, tokens)], 1
    )
    cols = rows.transpose(0, 2, 1)
    local_out, local_state = ssd_forward(conv_all, cols, rows)
    device_log = jnp.repeat(cumulative[-1], P_SIZE)
    zero_log = jnp.zeros(device_log.shape, jnp.float32)
    zero_state = jnp.zeros(local_state.shape, jnp.float32)
    state_in = prefix(
        (device_log, local_state), "seq", combine_states, (zero_log, zero_state), False
    )[1]
    ssd_out = local_out + decay_lane * lax.dot_general(
        c_rows, state_in, (((1,), (1,)), ((), ())), precision=highest
    )
    skip_lane = jnp.repeat(head_params[2], P_SIZE)[None, :]
    mixed_rows = ssd_out + skip_lane * inner_x
    gate_act = jax.nn.silu(gate_pre)
    gated_rows = mixed_rows * gate_act
    gate_gain = chan_params[K + 1]
    grad_mixed = jnp.dot(grad_rows, out_t, preferred_element_type=jnp.float32)
    gain_grad = grad_mixed * gate_gain[None, :]
    square_sum, cross_sum = lax.psum(
        jnp.stack([jnp.sum(gated_rows * gated_rows, -1), jnp.sum(gain_grad * gated_rows, -1)]),
        "head",
    )
    scaling_gate = lax.rsqrt(square_sum / DI + eps_norm)[:, None]
    mixed_b = (gated_rows * scaling_gate * gate_gain[None, :]).astype(half)
    out_partial = dot_last(mixed_b, out_t)
    out_sum = lax.psum(out_partial.astype(half), "head")
    g_out_t = lax.psum_scatter(
        dot_first(grad_rows, mixed_b).astype(half), shards, scatter_dimension=0, tiled=True
    ).astype(jnp.float32)
    grad_f = grad_rows.astype(jnp.float32)
    grad_gate_gain = jnp.sum(grad_mixed * gated_rows * scaling_gate, axis=0)
    grad_gated = scaling_gate * gain_grad - gated_rows * scaling_gate**3 * cross_sum[:, None] / DI
    grad_gate_b = (grad_gated * mixed_rows * silu_grad(gate_pre)).astype(half)
    grad_ssd = grad_gated * gate_act
    grad_skip = jnp.sum(jnp.sum(grad_ssd * inner_x, axis=0).reshape(head_local, P_SIZE), -1)
    grad_direct = lax.dot_general(
        grad_ssd * decay_lane, c_rows, (((0,), (0,)), ((), ())), precision=highest
    )
    grad_end = prefix(
        (device_log, grad_direct), "seq", combine_states, (zero_log, zero_state), True
    )[1]
    grad_x, grad_b, grad_c, grad_cols, grad_rows_dt = ssd_backward(
        conv_all, cols, rows, grad_ssd, state_in, grad_end
    )
    block_out = (block_f + out_sum.astype(jnp.float32)).astype(half)

    def per_head(values):
        return values.transpose(0, 2, 1).reshape(head_local, tokens)

    row_dt = grad_rows_dt.reshape(head_local, tokens)
    grad_dt_t = row_dt + per_head(grad_cols[:, :, 2:])
    steps_dt_t = rows[:, 2:].reshape(head_local, tokens)
    grad_cum_t = per_head(grad_cols[:, :, :2]) - row_dt * steps_dt_t
    grad_log_t = jnp.dot(grad_cum_t, lower, precision=highest)
    decay_rate = jnp.exp(head_params[1])[:, None]
    sigmoid_t = 1.0 - jnp.exp(-steps_dt_t)
    grad_step_t = (grad_dt_t - decay_rate * grad_log_t) * sigmoid_t
    grad_log_rate = -jnp.sum(grad_log_t * decay_rate * steps_dt_t, axis=1)
    grad_head = jnp.stack([jnp.sum(grad_step_t, axis=1), grad_log_rate, grad_skip])
    grad_act = jnp.concatenate([grad_x + skip_lane * grad_ssd, grad_b, grad_c], 1)
    grad_pre = grad_act * silu_grad(summed)
    edge_back = shifted(grad_pre[:edge_rows], "seq", -1)
    grad_ext = jnp.concatenate([grad_pre, edge_back], 0)
    grad_conv_b = sum(
        taps[k][None, :] * grad_ext[edge_rows - k : edge_rows - k + tokens] for k in range(K)
    ).astype(half)
    grad_taps = jnp.stack(
        [jnp.sum(padded[k : k + tokens] * grad_pre, axis=0) for k in range(K)]
        + [jnp.sum(grad_pre, axis=0)]
    )
    grad_inner_b = grad_conv_b[:, :inner_local]
    grad_bc_b = grad_conv_b[:, inner_local:]
    grad_step_b = grad_step_t.T.astype(half)
    both_b = jnp.concatenate([grad_gate_b, grad_inner_b], 1)
    grad_normed = (
        dot_last(both_b, zx_full)
        + jnp.dot(grad_bc_b, bc_t, preferred_element_type=jnp.float32)
        + dot_last(grad_step_b, dt_full)
    )
    bc_partial = dot_first(grad_bc_b, normed_b)
    bcconv_rows = jnp.pad(grad_taps[:, inner_local:], ((0, -(K + 1) % 8), (0, D - 2 * N)))
    stacked = jnp.concatenate([grad_normed, bc_partial, bcconv_rows], 0).astype(half)
    stacked = jnp.pad(stacked, ((0, -stacked.shape[0] % (16 * lax.axis_size("head"))), (0, 0)))
    summed_heads = head_sum(stacked).astype(jnp.float32)
    grad_normed = summed_heads[:tokens]
    row_block = D // lax.axis_size("head")
    bc_own = lax.dynamic_slice_in_dim(
        summed_heads[tokens : tokens + 2 * N], lax.axis_index("head") * row_block, row_block, 1
    )
    grad_in_cat = jnp.concatenate(
        [
            dot_first(normed_b, both_b),
            jnp.pad(dot_first(normed_b, grad_step_b), ((0, 0), (0, spare))),
        ],
        1,
    )
    g_in_cat = lax.psum_scatter(
        grad_in_cat.astype(half), shards, scatter_dimension=0, tiled=True
    ).astype(jnp.float32)
    scaled_grad = grad_normed * norm_gain[None, :]
    grad_norm_gain = jnp.sum(grad_normed * block_f * scaling_in, axis=0)
    in_rows = (
        grad_f
        + scaling_in * scaled_grad
        - block_f * scaling_in**3 * jnp.sum(scaled_grad * block_f, axis=-1, keepdims=True) / D
    )
    g_zx = jnp.stack([g_in_cat[:, :inner_local], g_in_cat[:, inner_local : 2 * inner_local]])
    g_dt = g_in_cat[:, 2 * inner_local : 2 * inner_local + head_local]
    g_out = g_out_t.T
    grad_chan = jnp.concatenate([grad_taps[:, :inner_local], grad_gate_gain[None, :]], 0)
    grad_bcconv = summed_heads[tokens + 2 * N : tokens + 2 * N + K + 1, : 2 * N]
    pieces = (grad_norm_gain, grad_chan, grad_head, grad_bcconv)
    flat = jnp.concatenate([piece.reshape(-1) for piece in pieces])
    flat = jnp.pad(flat, (0, -flat.shape[0] % (8 * 128))).reshape(-1, 128)
    small_sum, g_bc_t = shard_sum(flat, bc_own.reshape(D // shard_rows, -1, row_block))
    g_bc = g_bc_t.T
    small_sum = small_sum.reshape(-1)
    taken = []
    offset = 0
    for piece in pieces:
        taken.append(small_sum[offset : offset + piece.size].reshape(piece.shape))
        offset += piece.size
    g_gain, g_chan, g_head, g_bcconv = taken
    new_gain, nf_gain, ns_gain = adamw(
        norm_gain, g_gain, first_norm_gain, second_norm_gain, rate_vector, 0.0
    )
    new_zx, nf_zx, ns_zx = adamw(
        in_proj, g_zx, first_in_proj, second_in_proj, rate_matrix, decay_matrix
    )
    new_bc, nf_bc, ns_bc = adamw(
        bc_proj, g_bc, first_bc_proj, second_bc_proj, rate_matrix, decay_matrix
    )
    new_dt, nf_dt, ns_dt = adamw(
        dt_proj, g_dt, first_dt_proj, second_dt_proj, rate_matrix, decay_matrix
    )
    new_out, nf_out, ns_out = adamw(
        out_proj, g_out, first_out_proj, second_out_proj, rate_matrix, decay_matrix
    )
    new_chan, nf_chan, ns_chan = adamw(
        chan_params, g_chan, first_chan_params, second_chan_params, rate_vector, 0.0
    )
    new_head, nf_head, ns_head = adamw(
        head_params, g_head, first_head_params, second_head_params, rate_vector, 0.0
    )
    new_bcconv, nf_bcconv, ns_bcconv = adamw(
        bc_conv, g_bcconv, first_bc_conv, second_bc_conv, rate_vector, 0.0
    )
    return (
        block_out[None],
        in_rows[None],
        g_gain,
        g_zx,
        g_bc,
        g_dt,
        g_out,
        g_chan,
        g_head,
        g_bcconv,
        new_gain,
        new_zx,
        new_bc,
        new_dt,
        new_out,
        new_chan,
        new_head,
        new_bcconv,
        nf_gain,
        ns_gain,
        nf_zx,
        ns_zx,
        nf_bc,
        ns_bc,
        nf_dt,
        ns_dt,
        nf_out,
        ns_out,
        nf_chan,
        ns_chan,
        nf_head,
        ns_head,
        nf_bcconv,
        ns_bcconv,
    )


def solution(mesh):
    in_specs = (
        P("batch", "seq", None),
        P("batch", "seq", None),
        P(),
        P(None, ("seq", "batch"), "head"),
        P("head", ("seq", "batch")),
        P(("seq", "batch"), "head"),
        P("head", ("seq", "batch")),
        P(None, "head"),
        P(None, "head"),
        P(),
        P(),
        P(),
        P(None, ("seq", "batch"), "head"),
        P(None, ("seq", "batch"), "head"),
        P("head", ("seq", "batch")),
        P("head", ("seq", "batch")),
        P(("seq", "batch"), "head"),
        P(("seq", "batch"), "head"),
        P("head", ("seq", "batch")),
        P("head", ("seq", "batch")),
        P(None, "head"),
        P(None, "head"),
        P(None, "head"),
        P(None, "head"),
        P(),
        P(),
    )
    out_specs = (
        P("batch", "seq", None),
        P("batch", "seq", None),
        P(),
        P(None, ("seq", "batch"), "head"),
        P("head", ("seq", "batch")),
        P(("seq", "batch"), "head"),
        P("head", ("seq", "batch")),
        P(None, "head"),
        P(None, "head"),
        P(),
        P(),
        P(None, ("seq", "batch"), "head"),
        P("head", ("seq", "batch")),
        P(("seq", "batch"), "head"),
        P("head", ("seq", "batch")),
        P(None, "head"),
        P(None, "head"),
        P(),
        P(),
        P(),
        P(None, ("seq", "batch"), "head"),
        P(None, ("seq", "batch"), "head"),
        P("head", ("seq", "batch")),
        P("head", ("seq", "batch")),
        P(("seq", "batch"), "head"),
        P(("seq", "batch"), "head"),
        P("head", ("seq", "batch")),
        P("head", ("seq", "batch")),
        P(None, "head"),
        P(None, "head"),
        P(None, "head"),
        P(None, "head"),
        P(),
        P(),
    )
    return jax.shard_map(
        per_device, mesh=mesh, in_specs=in_specs, out_specs=out_specs, check_vma=False
    )
```
